32 devices in a mesh: dp: 4 (over y, x), ctx: 8 (over z, core).
Axes of the slice: x: 2, y: 2, z: 4, core: 2. Of those that a mesh axis runs over, the one named last changes fastest.
Arguments:
- block_input: bfloat16 [4, 1024, 896], P('dp', 'ctx'), may hold values from -6 to 6
- positions: int32 [4, 1024], P('dp', 'ctx'), may hold values from 0 to 1023, as said below
- cotangent: bfloat16 [4, 1024, 896], P('dp', 'ctx'), may hold values from -6 to 6
- norm1_gain: bfloat16 [896], P('ctx'), may hold values from 0.5 to 1.5
- w_query: bfloat16 [896, 896], P('dp', 'ctx'), may hold values from -5 to 5
- b_query: bfloat16 [896], P('ctx'), may hold values from -3 to 3
- w_key: bfloat16 [896, 128], P('dp', 'ctx'), may hold values from -1 to 1
- b_key: bfloat16 [128], P('ctx'), may hold values from -3 to 3
- w_value: bfloat16 [896, 128], P('dp', 'ctx'), may hold values from -0.1875 to 0.1875
- b_value: bfloat16 [128], P('ctx'), may hold values from -1 to 1
- w_out: bfloat16 [896, 896], P('dp', 'ctx'), may hold values from -0.75 to 0.75
- norm2_gain: bfloat16 [896], P('ctx'), may hold values from 0.5 to 1.5
- w_gate: bfloat16 [896, 4864], P('dp', 'ctx'), may hold values from -0.1875 to 0.1875
- w_up: bfloat16 [896, 4864], P('dp', 'ctx'), may hold values from -0.1875 to 0.1875
- w_down: bfloat16 [4864, 896], P('dp', 'ctx'), may hold values from -0.078125 to 0.078125
Outputs:
- block_output: bfloat16 [4, 1024, 896], P('dp', 'ctx')
- input_grad: float32 [4, 1024, 896], P('dp', 'ctx')
- grad_norm1: float32 [896], P('ctx')
- grad_w_query: float32 [896, 896], P('dp', 'ctx')
- grad_b_query: float32 [896], P('ctx')
- grad_w_key: float32 [896, 128], P('dp', 'ctx')
- grad_b_key: float32 [128], P('ctx')
- grad_w_value: float32 [896, 128], P('dp', 'ctx')
- grad_b_value: float32 [128], P('ctx')
- grad_w_out: float32 [896, 896], P('dp', 'ctx')
- grad_norm2: float32 [896], P('ctx')
- grad_w_gate: float32 [896, 4864], P('dp', 'ctx')
- grad_w_up: float32 [896, 4864], P('dp', 'ctx')
- grad_w_down: float32 [4864, 896], P('dp', 'ctx')
The draws below stay inside these ranges and needn't reach their ends.
Inputs may be any that keep to these rules, and one draw needn't show every extreme that they name: In every sequence, stored tokens 64 * j to 64 * (j + 1) - 1 have the positions 64 * m to 64 * (m + 1) - 1 in ascending order, each m for exactly one j.
All inputs are finite; a program needn't handle non-finite values.
Results may differ from the reference program's by a relative error of at most 0.02.
Values may be sent and summed in bfloat16 or wider, within the bound.
A program may use at most 192 MiB of HBM per device.

```python
import jax
import jax.numpy as jnp
from jax import lax

D = 896
HEADS = 14
KV_HEADS = 2
HEAD = 64
FF = 4864
TOK_DEV = 128
RUN = 64
SEQ = 1024
NSEQ = 4
QW = 896
KVW = 128
GROUP = 7


def projection_pair(key):
    base = jax.random.fold_in(key, 5)
    first_key, second_key = jax.random.split(base, 2)
    key_weights = jax.random.truncated_normal(first_key, -6.0, 6.0, (D, KV_HEADS * HEAD), jnp.float32) * D ** (-0.5)
    query_weights = jax.random.truncated_normal(second_key, -6.0, 6.0, (D, HEADS * HEAD), jnp.float32) * D ** (-0.5)
    return (query_weights, key_weights)


def draw_w_query(key, part):
    query_weights, key_weights = projection_pair(key)
    return query_weights.astype(jnp.bfloat16)


def draw_w_key(key, part):
    query_weights, key_weights = projection_pair(key)
    return key_weights.astype(jnp.bfloat16)


def draw_positions(key, part):
    run_count = SEQ // RUN
    seq_keys = jax.random.split(jax.random.fold_in(key, 3), NSEQ)

    def one_order(seq_key):
        return jax.random.permutation(seq_key, run_count).astype(jnp.int32)
    orders = jax.vmap(one_order)(seq_keys)
    slot = jnp.arange(SEQ, dtype=jnp.int32)
    return (orders[:, slot // RUN] * RUN + slot % RUN).astype(jnp.int32)


def shard_levels(stream_key, extent, shards, low, top_value):
    def one(dim, parts):
        heights = jax.random.uniform(jax.random.fold_in(jax.random.fold_in(stream_key, 6), dim), (parts,), jnp.float32, low / len(shards), top_value / len(shards))
        return jnp.repeat(jnp.exp(heights), extent[dim] // parts).reshape((-1,) + (1,) * (len(extent) - dim - 1))

    loudness = one(*shards[0])
    for cut in shards[1:]:
        loudness = loudness * one(*cut)
    return loudness


def normal_values(own_key, dims, spread, limit, cuts=(), kind=jnp.bfloat16):
    array = jax.random.normal(own_key, dims, jnp.float32) * spread
    if len(cuts) > 0:
        array = shard_levels(own_key, dims, cuts, -0.22, 0.18) * array
    return jnp.clip(array, min=-limit, max=limit).astype(kind)


def setup_inputs(seed: int = 0) -> dict:
    streams_of = jax.random.split(jax.random.key(seed), 16)
    block_input = normal_values(streams_of[0], (NSEQ, SEQ, D), 1.0, 6.0, ((0, 4), (1, 8)))
    positions = draw_positions(jax.random.fold_in(streams_of[15], 71), 0)
    cotangent = normal_values(streams_of[2], (NSEQ, SEQ, D), 1.0, 6.0, ((0, 4), (1, 8)))
    norm1_gain = jnp.clip(1.0 + 0.1 * jax.random.normal(streams_of[3], (D,), jnp.float32), 0.5, 1.5).astype(jnp.bfloat16)
    w_query = draw_w_query(jax.random.fold_in(streams_of[15], 71), 0)
    b_query = normal_values(streams_of[5], (QW,), 0.5, 3.0, ((0, 8),))
    w_key = draw_w_key(jax.random.fold_in(streams_of[15], 71), 0)
    b_key = normal_values(streams_of[7], (KVW,), 0.5, 3.0, ((0, 8),))
    w_value = normal_values(streams_of[8], (D, KVW), D ** -0.5, 0.1875, ((0, 4), (1, 8)))
    b_value = normal_values(streams_of[9], (KVW,), 0.15, 1.0, ((0, 8),))
    w_out = normal_values(streams_of[10], (QW, D), 64 ** -0.5, 0.75, ((0, 4), (1, 8)))
    norm2_gain = jnp.clip(1.0 + 0.1 * jax.random.normal(streams_of[11], (D,), jnp.float32), 0.5, 1.5).astype(jnp.bfloat16)
    w_gate = normal_values(streams_of[12], (D, FF), D ** -0.5, 0.1875, ((0, 4), (1, 8)))
    w_up = normal_values(streams_of[13], (D, FF), D ** -0.5, 0.1875, ((0, 4), (1, 8)))
    w_down = normal_values(streams_of[14], (FF, D), FF ** -0.5, 0.078125, ((0, 4), (1, 8)))
    return dict(block_input=block_input, positions=positions, cotangent=cotangent, norm1_gain=norm1_gain, w_query=w_query, b_query=b_query, w_key=w_key, b_key=b_key, w_value=w_value, b_value=b_value, w_out=w_out, norm2_gain=norm2_gain, w_gate=w_gate, w_up=w_up, w_down=w_down)


EPSILON = 1e-06
THETA = 1000000.0

def rms_parts(values):
    inverse = lax.rsqrt(lax.optimization_barrier(jnp.mean(values * values, axis=-1, keepdims=True)) + EPSILON)
    return (values * inverse, inverse)

def rms_back(grads, normed, inverse):
    return inverse * (grads - normed * lax.optimization_barrier(jnp.mean(grads * normed, axis=-1, keepdims=True)))

def rotary(places):
    half_size = HEAD // 2
    freq = THETA ** (-(jnp.arange(half_size).astype(jnp.float32) * 2.0 / HEAD))
    angle = places.astype(jnp.float32)[:, None] * freq[None, :]
    cosine = jnp.cos(angle)
    sine = jnp.sin(angle)
    return (jnp.concatenate([cosine, cosine], 1)[:, None, :], jnp.concatenate([sine, sine], 1)[:, None, :])

def turn_half(values):
    half_size = values.shape[-1] // 2
    return jnp.concatenate([-values[..., half_size:], values[..., :half_size]], axis=-1)

def rotate(values, cosine, sine):
    return values * cosine + turn_half(values) * sine

def unrotate(grads, cosine, sine):
    return grads * cosine - turn_half(grads) * sine

def rounded(values):
    return lax.optimization_barrier(values.astype(jnp.bfloat16)).astype(jnp.float32)

def attend_forward(queries, query_pos, keys_sorted, values_sorted, blocks, width, scaling):
    row_count, kv_count, group_size, head_size = queries.shape
    query_f = queries.astype(jnp.float32)

    def advance(index_block, carry):
        running_max, running_sum, weighted = carry
        first = index_block * width
        block_keys = lax.dynamic_slice_in_dim(keys_sorted, first, width, 0).astype(jnp.float32)
        block_values = lax.dynamic_slice_in_dim(values_sorted, first, width, 0).astype(jnp.float32)
        key_pos = first + jnp.arange(width, dtype=jnp.int32)
        scores = jnp.einsum('qkgd,skd->kgqs', query_f, block_keys) * scaling
        scores = jnp.where(key_pos[None, :] <= query_pos[:, None], scores, -jnp.inf)
        new_max = jnp.maximum(running_max, lax.optimization_barrier(jnp.max(scores, axis=-1)))
        rescale = jnp.exp(running_max - new_max)
        exponent = jnp.exp(scores - new_max[..., None])
        running_sum = running_sum * rescale + lax.optimization_barrier(jnp.sum(exponent, axis=-1))
        weighted = weighted * rescale[..., None] + jnp.einsum('kgqs,skd->kgqd', rounded(exponent), block_values)
        return (new_max, running_sum, weighted)
    start_state = (jnp.full((kv_count, group_size, row_count), -jnp.inf, jnp.float32), jnp.zeros((kv_count, group_size, row_count), jnp.float32), jnp.zeros((kv_count, group_size, row_count, head_size), jnp.float32))
    running_max, running_sum, weighted = lax.fori_loop(0, blocks, advance, start_state)
    return (weighted / running_sum[..., None], running_max + jnp.log(running_sum))

def attend_backward(queries, query_pos, keys_sorted, values_sorted, grad_out, out_rows, log_total, blocks, width, scaling, key_grads, value_grads):
    query_f = queries.astype(jnp.float32)
    grad_f = grad_out.astype(jnp.float32)
    delta_rows = lax.optimization_barrier(jnp.sum(grad_f * out_rows.astype(jnp.float32), axis=-1))

    def advance(index_block, carry):
        query_grad, key_acc, value_acc = carry
        first = index_block * width
        block_keys = lax.dynamic_slice_in_dim(keys_sorted, first, width, 0).astype(jnp.float32)
        block_values = lax.dynamic_slice_in_dim(values_sorted, first, width, 0).astype(jnp.float32)
        key_pos = first + jnp.arange(width, dtype=jnp.int32)
        scores = jnp.einsum('qkgd,skd->kgqs', query_f, block_keys) * scaling
        scores = jnp.where(key_pos[None, :] <= query_pos[:, None], scores, -jnp.inf)
        prob = jnp.exp(scores - log_total[..., None])
        value_part = jnp.einsum('kgqs,kgqd->skd', rounded(prob), grad_f)
        prob_grad = jnp.einsum('kgqd,skd->kgqs', grad_f, block_values)
        score_grad = rounded(prob * (prob_grad - delta_rows[..., None]) * scaling)
        query_grad = query_grad + jnp.einsum('kgqs,skd->kgqd', score_grad, block_keys)
        key_part = jnp.einsum('kgqs,qkgd->skd', score_grad, query_f)
        key_acc = lax.dynamic_update_slice_in_dim(key_acc, lax.dynamic_slice_in_dim(key_acc, first, width, 0) + key_part, first, 0)
        value_acc = lax.dynamic_update_slice_in_dim(value_acc, lax.dynamic_slice_in_dim(value_acc, first, width, 0) + value_part, first, 0)
        return (query_grad, key_acc, value_acc)
    row_count, kv_count, group_size, head_size = queries.shape
    start_state = (jnp.zeros((kv_count, group_size, row_count, head_size), jnp.float32), key_grads, value_grads)
    return lax.fori_loop(0, blocks, advance, start_state)

def reference(block_input, positions, cotangent, norm1_gain, w_query, b_query, w_key, b_key, w_value, b_value, w_out, norm2_gain, w_gate, w_up, w_down):
    f32 = jnp.float32
    bf16 = jnp.bfloat16
    scaling = HEAD ** (-0.5)
    q_block = 512 if SEQ % 512 == 0 else SEQ
    gain_one = norm1_gain.astype(f32)
    gain_two = norm2_gain.astype(f32)

    def sequence_step(totals, slices):
        inputs_b, place, cot_b = slices
        order_index = jnp.argsort(place).astype(jnp.int32)
        inputs = inputs_b[order_index].astype(f32)
        cot_sorted = cot_b[order_index]
        natural = jnp.arange(SEQ, dtype=jnp.int32)
        normed_one, inverse_one = rms_parts(inputs)
        act_one = (normed_one * gain_one).astype(bf16)
        queries = jnp.dot(act_one, w_query, preferred_element_type=f32) + b_query.astype(f32)
        keys = jnp.dot(act_one, w_key, preferred_element_type=f32) + b_key.astype(f32)
        values = jnp.dot(act_one, w_value, preferred_element_type=f32) + b_value.astype(f32)
        cosine, sine = rotary(natural)
        query_rot = rotate(queries.reshape(SEQ, HEADS, HEAD), cosine, sine).astype(bf16)
        key_rot = rotate(keys.reshape(SEQ, KV_HEADS, HEAD), cosine, sine).astype(bf16)
        value_b = values.reshape(SEQ, KV_HEADS, HEAD).astype(bf16)
        pieces = []
        log_totals = []
        for index_query in range(SEQ // q_block):
            lower = index_query * q_block
            row_block = query_rot[lower:lower + q_block].reshape(q_block, KV_HEADS, GROUP, HEAD)
            blocks = (lower + q_block - 1) // TOK_DEV + 1
            mixed, log_total = attend_forward(row_block, natural[lower:lower + q_block], key_rot, value_b, blocks, TOK_DEV, scaling)
            pieces.append(jnp.transpose(mixed, (2, 0, 1, 3)).reshape(q_block, HEADS * HEAD))
            log_totals.append(log_total)
        attended = jnp.concatenate(pieces, 0).astype(bf16)
        residual = inputs + jnp.dot(attended, w_out, preferred_element_type=f32)
        normed_two, inverse_two = rms_parts(residual)
        act_two = (normed_two * gain_two).astype(bf16)
        gate = jnp.dot(act_two, w_gate, preferred_element_type=f32)
        up_proj = jnp.dot(act_two, w_up, preferred_element_type=f32)
        sigmoid_gate = jax.nn.sigmoid(gate)
        silu_gate = gate * sigmoid_gate
        hidden = (silu_gate * up_proj).astype(bf16)
        output = (residual + jnp.dot(hidden, w_down, preferred_element_type=f32)).astype(bf16)
        grad_down = jnp.dot(hidden.T, cot_sorted, preferred_element_type=f32)
        hidden_grad = jnp.dot(cot_sorted, w_down.T, preferred_element_type=f32)
        gate_grad = (hidden_grad * up_proj * sigmoid_gate * (1.0 + gate * (1.0 - sigmoid_gate))).astype(bf16)
        up_grad = (hidden_grad * silu_gate).astype(bf16)
        grad_gate = jnp.dot(act_two.T, gate_grad, preferred_element_type=f32)
        grad_up = jnp.dot(act_two.T, up_grad, preferred_element_type=f32)
        act_two_grad = jnp.dot(gate_grad, w_gate.T, preferred_element_type=f32) + jnp.dot(up_grad, w_up.T, preferred_element_type=f32)
        grad_gain_two = lax.optimization_barrier(jnp.sum(act_two_grad * normed_two, axis=0))
        residual_grad = cot_sorted.astype(f32) + rms_back(act_two_grad * gain_two, normed_two, inverse_two)
        residual_b = residual_grad.astype(bf16)
        grad_out_w = jnp.dot(attended.T, residual_b, preferred_element_type=f32)
        attended_grad = jnp.dot(residual_b, w_out.T, preferred_element_type=f32).astype(bf16)
        key_grads = jnp.zeros((SEQ, KV_HEADS, HEAD), f32)
        value_grads = jnp.zeros((SEQ, KV_HEADS, HEAD), f32)
        query_parts = []
        for index_query in range(SEQ // q_block):
            lower = index_query * q_block
            row_block = query_rot[lower:lower + q_block].reshape(q_block, KV_HEADS, GROUP, HEAD)
            blocks = (lower + q_block - 1) // TOK_DEV + 1
            grad_rows = jnp.transpose(attended_grad[lower:lower + q_block].reshape(q_block, KV_HEADS, GROUP, HEAD), (1, 2, 0, 3))
            out_rows = jnp.transpose(attended[lower:lower + q_block].reshape(q_block, KV_HEADS, GROUP, HEAD), (1, 2, 0, 3))
            query_grad, key_grads, value_grads = attend_backward(row_block, natural[lower:lower + q_block], key_rot, value_b, grad_rows, out_rows, log_totals[index_query], blocks, TOK_DEV, scaling, key_grads, value_grads)
            query_parts.append(jnp.transpose(query_grad, (2, 0, 1, 3)))
        query_grad = unrotate(jnp.concatenate(query_parts, 0).reshape(SEQ, HEADS, HEAD), cosine, sine).reshape(SEQ, HEADS * HEAD)
        key_grad = unrotate(key_grads, cosine, sine).reshape(SEQ, KV_HEADS * HEAD)
        value_grad = value_grads.reshape(SEQ, KV_HEADS * HEAD)
        query_b = query_grad.astype(bf16)
        key_b = key_grad.astype(bf16)
        value_gb = value_grad.astype(bf16)
        grad_wq = jnp.dot(act_one.T, query_b, preferred_element_type=f32)
        grad_wk = jnp.dot(act_one.T, key_b, preferred_element_type=f32)
        grad_wv = jnp.dot(act_one.T, value_gb, preferred_element_type=f32)
        act_one_grad = jnp.dot(query_b, w_query.T, preferred_element_type=f32) + jnp.dot(key_b, w_key.T, preferred_element_type=f32) + jnp.dot(value_gb, w_value.T, preferred_element_type=f32)
        grad_gain_one = lax.optimization_barrier(jnp.sum(act_one_grad * normed_one, axis=0))
        input_grad = residual_grad + rms_back(act_one_grad * gain_one, normed_one, inverse_one)
        terms = (grad_gain_one, grad_wq, lax.optimization_barrier(jnp.sum(query_grad, axis=0)), grad_wk, lax.optimization_barrier(jnp.sum(key_grad, axis=0)), grad_wv, lax.optimization_barrier(jnp.sum(value_grad, axis=0)), grad_out_w, grad_gain_two, grad_gate, grad_up, grad_down)
        totals = jax.tree.map(jnp.add, totals, terms)
        return (totals, (output[place], input_grad[place]))
    start_totals = (jnp.zeros((D,), f32), jnp.zeros((D, QW), f32), jnp.zeros((QW,), f32), jnp.zeros((D, KVW), f32), jnp.zeros((KVW,), f32), jnp.zeros((D, KVW), f32), jnp.zeros((KVW,), f32), jnp.zeros((QW, D), f32), jnp.zeros((D,), f32), jnp.zeros((D, FF), f32), jnp.zeros((D, FF), f32), jnp.zeros((FF, D), f32))
    totals, stacked = lax.scan(sequence_step, start_totals, (block_input, positions, cotangent))
    outputs, input_grads = stacked
    return (outputs, input_grads, totals[0], totals[1], totals[2], totals[3], totals[4], totals[5], totals[6], totals[7], totals[8], totals[9], totals[10], totals[11])
```

```python
import jax
import jax.numpy as jnp
from jax import lax
from jax.sharding import PartitionSpec as P

HEADS = 14
KV_HEADS = 2
HEAD = 64
GROUP = 7


EPSILON = 1e-06
THETA = 1000000.0


def rms_parts(values):
    inverse = lax.rsqrt(jnp.mean(values * values, axis=-1, keepdims=True) + EPSILON)
    return (values * inverse, inverse)


def rms_back(grads, normed, inverse):
    return inverse * (grads - normed * jnp.mean(grads * normed, axis=-1, keepdims=True))


def rotary(places):
    half_size = HEAD // 2
    freq = THETA ** (-(jnp.arange(half_size).astype(jnp.float32) * 2.0 / HEAD))
    angle = places.astype(jnp.float32)[:, None] * freq[None, :]
    cosine = jnp.cos(angle)
    sine = jnp.sin(angle)
    return (
        jnp.concatenate([cosine, cosine], 1)[:, None, :],
        jnp.concatenate([sine, sine], 1)[:, None, :],
    )


def turn_half(values):
    half_size = values.shape[-1] // 2
    return jnp.concatenate([-values[..., half_size:], values[..., :half_size]], axis=-1)


def rotate(values, cosine, sine):
    return values * cosine + turn_half(values) * sine


def unrotate(grads, cosine, sine):
    return grads * cosine - turn_half(grads) * sine


def gather(block, axes):
    return lax.all_gather(block, axes, axis=0, tiled=False)


def exchange(blocks, axis):
    return lax.all_to_all(blocks, axis, split_axis=0, concat_axis=0, tiled=True)


def summed_scatter(blocks, axis):
    return lax.psum_scatter(blocks, axis, scatter_dimension=0, tiled=False)


def attend_forward(queries, query_pos, keys_sorted, values_sorted, blocks, width, scaling):
    row_count, kv_count, group_size, head_size = queries.shape

    def advance(index_block, carry):
        running_max, running_sum, weighted = carry
        first = index_block * width
        block_keys = lax.dynamic_slice_in_dim(keys_sorted, first, width, 0)
        block_values = lax.dynamic_slice_in_dim(values_sorted, first, width, 0)
        key_pos = first + jnp.arange(width, dtype=jnp.int32)
        scores = (
            jnp.einsum("qkgd,skd->kgqs", queries, block_keys, preferred_element_type=jnp.float32)
            * scaling
        )
        scores = jnp.where(key_pos[None, :] <= query_pos[:, None], scores, -jnp.inf)
        new_max = jnp.maximum(running_max, jnp.max(scores, axis=-1))
        rescale = jnp.exp(running_max - new_max)
        exponent = jnp.exp(scores - new_max[..., None])
        running_sum = running_sum * rescale + jnp.sum(exponent, axis=-1)
        weighted = weighted * rescale[..., None] + jnp.einsum(
            "kgqs,skd->kgqd",
            exponent.astype(jnp.bfloat16),
            block_values,
            preferred_element_type=jnp.float32,
        )
        return (new_max, running_sum, weighted)

    start_state = (
        jnp.full((kv_count, group_size, row_count), -jnp.inf, jnp.float32),
        jnp.zeros((kv_count, group_size, row_count), jnp.float32),
        jnp.zeros((kv_count, group_size, row_count, head_size), jnp.float32),
    )
    running_max, running_sum, weighted = lax.fori_loop(0, blocks, advance, start_state)
    return (weighted / running_sum[..., None], running_max + jnp.log(running_sum))


def attend_backward(
    queries,
    query_pos,
    keys_sorted,
    values_sorted,
    grad_out,
    out_rows,
    log_total,
    blocks,
    width,
    scaling,
    key_grads,
    value_grads,
):
    delta_rows = jnp.sum(grad_out.astype(jnp.float32) * out_rows.astype(jnp.float32), axis=-1)

    def advance(index_block, carry):
        query_grad, key_acc, value_acc = carry
        first = index_block * width
        block_keys = lax.dynamic_slice_in_dim(keys_sorted, first, width, 0)
        block_values = lax.dynamic_slice_in_dim(values_sorted, first, width, 0)
        key_pos = first + jnp.arange(width, dtype=jnp.int32)
        scores = (
            jnp.einsum("qkgd,skd->kgqs", queries, block_keys, preferred_element_type=jnp.float32)
            * scaling
        )
        scores = jnp.where(key_pos[None, :] <= query_pos[:, None], scores, -jnp.inf)
        prob = jnp.exp(scores - log_total[..., None])
        value_part = jnp.einsum(
            "kgqs,kgqd->skd",
            prob.astype(jnp.bfloat16),
            grad_out,
            preferred_element_type=jnp.float32,
        )
        prob_grad = jnp.einsum(
            "kgqd,skd->kgqs", grad_out, block_values, preferred_element_type=jnp.float32
        )
        score_grad = (prob * (prob_grad - delta_rows[..., None]) * scaling).astype(jnp.bfloat16)
        query_grad = query_grad + jnp.einsum(
            "kgqs,skd->kgqd", score_grad, block_keys, preferred_element_type=jnp.float32
        )
        key_part = jnp.einsum(
            "kgqs,qkgd->skd", score_grad, queries, preferred_element_type=jnp.float32
        )
        key_acc = lax.dynamic_update_slice_in_dim(
            key_acc, lax.dynamic_slice_in_dim(key_acc, first, width, 0) + key_part, first, 0
        )
        value_acc = lax.dynamic_update_slice_in_dim(
            value_acc, lax.dynamic_slice_in_dim(value_acc, first, width, 0) + value_part, first, 0
        )
        return (query_grad, key_acc, value_acc)

    row_count, kv_count, group_size, head_size = queries.shape
    start_state = (
        jnp.zeros((kv_count, group_size, row_count, head_size), jnp.float32),
        key_grads,
        value_grads,
    )
    return lax.fori_loop(0, blocks, advance, start_state)


def rows_to_columns(w_down, data_count, ctx_count):
    ratio = ctx_count // data_count
    rows = w_down.shape[0] // ratio
    low = lax.rem(lax.axis_index("ctx"), ratio)
    arrived = []
    for turn in range(ratio):
        pairs = [
            (a * ctx_count + ratio * d + e, d * ctx_count + ratio * a + (e + turn) % ratio)
            for a in range(data_count)
            for d in range(data_count)
            for e in range(ratio)
        ]
        block = lax.rem(low + turn, ratio)
        piece = lax.dynamic_slice_in_dim(w_down, block * rows, rows, 0)
        arrived.append(lax.ppermute(piece, ("dp", "ctx"), pairs))
    stacked = jnp.stack(arrived, 0)
    order = lax.rem(low - jnp.arange(ratio, dtype=jnp.int32) + ratio, ratio)
    stacked = stacked[order]
    return jnp.transpose(stacked, (1, 0, 2)).reshape(rows, -1)


def columns_to_rows(grad, data_count, ctx_count):
    ratio = ctx_count // data_count
    rows, columns = grad.shape
    width = columns // ratio
    low = lax.rem(lax.axis_index("ctx"), ratio)
    arrived = []
    for turn in range(ratio):
        pairs = [
            (d * ctx_count + ratio * a + (e + turn) % ratio, a * ctx_count + ratio * d + e)
            for a in range(data_count)
            for d in range(data_count)
            for e in range(ratio)
        ]
        block = lax.rem(low - turn + ratio, ratio)
        piece = lax.dynamic_slice_in_dim(grad, block * width, width, 1)
        arrived.append(lax.ppermute(piece, ("dp", "ctx"), pairs))
    order = lax.rem(low + jnp.arange(ratio, dtype=jnp.int32), ratio)
    placed = jnp.zeros((ratio, rows, width), grad.dtype)
    for turn in range(ratio):
        placed = lax.dynamic_update_slice_in_dim(placed, arrived[turn][None], order[turn], 0)
    return placed.reshape(ratio * rows, width)


def split_sum(values):
    high = values.astype(jnp.bfloat16)
    low = (values - high.astype(jnp.float32)).astype(jnp.bfloat16)
    return high, low


def per_device(
    block_input,
    positions,
    cotangent,
    norm1_gain,
    w_query,
    b_query,
    w_key,
    b_key,
    w_value,
    b_value,
    w_out,
    norm2_gain,
    w_gate,
    w_up,
    w_down,
):
    f32 = jnp.float32
    bf16 = jnp.bfloat16
    tokens, model = block_input.shape[1:]
    half_rows = tokens // 2
    ctx_count = lax.axis_size("ctx")
    data_count = lax.axis_size("dp")
    run_count = 2 * ctx_count
    seq_length = tokens * ctx_count
    kv_width = KV_HEADS * HEAD
    scaling = HEAD ** (-0.5)
    inputs = block_input[0].astype(f32)
    place = positions[0]
    cot_local = cotangent[0]
    starts = place.reshape(2, half_rows)[:, 0]
    in_rows = w_query.shape[0]
    q_cols = w_query.shape[1]
    k_cols = w_key.shape[1]
    o_cols = w_out.shape[1]
    wide = q_cols + 2 * k_cols + o_cols
    runs_row = jnp.pad((starts // half_rows).astype(bf16), (0, wide - 2))
    gain_row = jnp.pad(norm2_gain, (0, wide - norm2_gain.shape[0]))
    vectors = jnp.stack(
        [jnp.concatenate([b_query, b_key, b_value, norm1_gain]), gain_row, runs_row]
    )
    vectors = jnp.pad(vectors, ((0, 13), (0, 0)))
    packed = jnp.concatenate(
        [jnp.concatenate([w_query, w_key, w_value, w_out], 1), vectors], 0
    )
    everything = gather(packed, ("dp", "ctx"))
    everything = everything.reshape(data_count, ctx_count, in_rows + 16, wide)

    def columns_of(lower, width):
        part = everything[:, :, :in_rows, lower : lower + width]
        return jnp.transpose(part, (0, 2, 1, 3)).reshape(data_count * in_rows, ctx_count * width)

    full_wq = columns_of(0, q_cols)
    full_wk = columns_of(q_cols, k_cols)
    full_wv = columns_of(q_cols + k_cols, k_cols)
    full_wo = columns_of(q_cols + 2 * k_cols, o_cols)
    data_index = lax.axis_index("dp")
    mine = lax.dynamic_index_in_dim(everything[:, :, in_rows:, :], data_index, 0, keepdims=False)
    full_bq = mine[:, 0, :q_cols].reshape(-1)
    full_bk = mine[:, 0, q_cols : q_cols + k_cols].reshape(-1)
    full_bv = mine[:, 0, q_cols + k_cols : q_cols + 2 * k_cols].reshape(-1)
    gain_one = mine[:, 0, q_cols + 2 * k_cols :].reshape(-1).astype(f32)
    gain_two = mine[:, 1, : norm2_gain.shape[0]].reshape(-1).astype(f32)
    ranking = mine[:, 2, :2].reshape(-1).astype(jnp.int32)

    gate_up = gather(jnp.concatenate([w_gate, w_up], 1), "dp").reshape(model, -1)
    units = w_gate.shape[1]
    my_gate = gate_up[:, :units]
    my_up = gate_up[:, units:]
    my_down = gather(rows_to_columns(w_down, data_count, ctx_count), "dp")
    my_down = jnp.transpose(my_down, (1, 0, 2)).reshape(units, model)
    cot_all = gather(cot_local, "ctx").reshape(seq_length, model)

    normed_one, inverse_one = rms_parts(inputs)
    act_one = (normed_one * gain_one).astype(bf16)
    queries = jnp.dot(act_one, full_wq, preferred_element_type=f32) + full_bq.astype(f32)
    keys = jnp.dot(act_one, full_wk, preferred_element_type=f32) + full_bk.astype(f32)
    values = jnp.dot(act_one, full_wv, preferred_element_type=f32) + full_bv.astype(f32)
    cosine, sine = rotary(place)
    query_rot = rotate(queries.reshape(tokens, HEADS, HEAD), cosine, sine).astype(bf16)
    key_rot = (
        rotate(keys.reshape(tokens, KV_HEADS, HEAD), cosine, sine)
        .astype(bf16)
        .reshape(tokens, kv_width)
    )
    value_b = values.astype(bf16)
    both_all = gather(jnp.concatenate([key_rot, value_b], 1), "ctx")
    run_index = jnp.arange(run_count, dtype=jnp.int32)
    owners = jnp.sum(
        jnp.where(ranking[None, :] == run_index[:, None], run_index[None, :], 0), axis=1
    )
    both_sorted = both_all.reshape(run_count, half_rows, 2 * kv_width)[owners].reshape(
        seq_length, 2, KV_HEADS, HEAD
    )
    keys_sorted = both_sorted[:, 0]
    values_sorted = both_sorted[:, 1]
    pieces = []
    log_totals = []
    block_counts = []
    for index_run in range(2):
        lower = index_run * half_rows
        row_block = query_rot[lower : lower + half_rows].reshape(half_rows, KV_HEADS, GROUP, HEAD)
        blocks = starts[index_run] // tokens + 1
        mixed, log_total = attend_forward(
            row_block,
            place[lower : lower + half_rows],
            keys_sorted,
            values_sorted,
            blocks,
            tokens,
            scaling,
        )
        pieces.append(jnp.transpose(mixed, (2, 0, 1, 3)).reshape(half_rows, HEADS * HEAD))
        log_totals.append(log_total)
        block_counts.append(blocks)
    attended = jnp.concatenate(pieces, 0).astype(bf16)
    residual = inputs + jnp.dot(attended, full_wo, preferred_element_type=f32)
    normed_two, inverse_two = rms_parts(residual)
    act_two = (normed_two * gain_two).astype(bf16)
    act_two_all = gather(act_two, "ctx").reshape(seq_length, model)
    saved_all = gather(jnp.concatenate([act_one, attended], 1), "ctx")
    saved_all = saved_all.reshape(seq_length, model + HEADS * HEAD)

    gate = jnp.dot(act_two_all, my_gate, preferred_element_type=f32)
    up_proj = jnp.dot(act_two_all, my_up, preferred_element_type=f32)
    sigmoid_gate = jax.nn.sigmoid(gate)
    silu_gate = gate * sigmoid_gate
    hidden = (silu_gate * up_proj).astype(bf16)
    out_part = jnp.dot(hidden, my_down, preferred_element_type=f32).astype(bf16)
    hidden_grad = jnp.dot(cot_all, my_down.T, preferred_element_type=f32)
    gate_grad = (hidden_grad * up_proj * sigmoid_gate * (1.0 + gate * (1.0 - sigmoid_gate))).astype(
        bf16
    )
    up_grad = (hidden_grad * silu_gate).astype(bf16)
    act_part = (
        jnp.dot(gate_grad, my_gate.T, preferred_element_type=f32)
        + jnp.dot(up_grad, my_up.T, preferred_element_type=f32)
    ).astype(bf16)
    parts = jnp.concatenate([out_part, act_part], 1).reshape(ctx_count, tokens, 2 * model)
    arrived = summed_scatter(parts, "ctx").astype(f32)
    output = (residual + arrived[:, :model]).astype(bf16)
    act_two_grad = arrived[:, model:]

    grad_gate = jnp.dot(act_two_all.T, gate_grad, preferred_element_type=f32).astype(bf16)
    grad_up = jnp.dot(act_two_all.T, up_grad, preferred_element_type=f32).astype(bf16)
    grad_down = jnp.dot(hidden.T, cot_all, preferred_element_type=f32).astype(bf16)
    gate_up_grad = jnp.concatenate([grad_gate, grad_up], 1).reshape(data_count, -1, 2 * units)
    gate_up_grad = summed_scatter(gate_up_grad, "dp").astype(f32)
    down_grad = jnp.transpose(grad_down.reshape(units, data_count, -1), (1, 0, 2))
    down_grad = summed_scatter(down_grad, "dp")
    down_grad = columns_to_rows(down_grad, data_count, ctx_count).astype(f32)

    grad_gain_two = jnp.sum(act_two_grad * normed_two, axis=0)
    residual_grad = cot_local.astype(f32) + rms_back(
        act_two_grad * gain_two, normed_two, inverse_two
    )
    residual_b = residual_grad.astype(bf16)
    attended_grad = jnp.dot(residual_b, full_wo.T, preferred_element_type=f32).astype(bf16)
    key_grads = jnp.zeros((seq_length, KV_HEADS, HEAD), f32)
    value_grads = jnp.zeros((seq_length, KV_HEADS, HEAD), f32)
    query_parts = []
    for index_run in range(2):
        lower = index_run * half_rows
        row_block = query_rot[lower : lower + half_rows].reshape(half_rows, KV_HEADS, GROUP, HEAD)
        grad_rows = jnp.transpose(
            attended_grad[lower : lower + half_rows].reshape(half_rows, KV_HEADS, GROUP, HEAD),
            (1, 2, 0, 3),
        )
        out_rows = jnp.transpose(
            attended[lower : lower + half_rows].reshape(half_rows, KV_HEADS, GROUP, HEAD),
            (1, 2, 0, 3),
        )
        query_grad, key_grads, value_grads = attend_backward(
            row_block,
            place[lower : lower + half_rows],
            keys_sorted,
            values_sorted,
            grad_rows,
            out_rows,
            log_totals[index_run],
            block_counts[index_run],
            tokens,
            scaling,
            key_grads,
            value_grads,
        )
        query_parts.append(jnp.transpose(query_grad, (2, 0, 1, 3)))
    slots = jnp.concatenate(
        [key_grads.reshape(seq_length, kv_width), value_grads.reshape(seq_length, kv_width)], 1
    )
    slots = slots.reshape(run_count, half_rows, 2 * kv_width)[ranking]
    both_local = summed_scatter(slots.reshape(ctx_count, tokens, 2 * kv_width), "ctx")
    key_local = both_local[:, :kv_width]
    value_local = both_local[:, kv_width:]
    query_grad = unrotate(
        jnp.concatenate(query_parts, 0).reshape(tokens, HEADS, HEAD), cosine, sine
    ).reshape(tokens, HEADS * HEAD)
    key_grad = unrotate(key_local.reshape(tokens, KV_HEADS, HEAD), cosine, sine).reshape(
        tokens, kv_width
    )
    query_b = query_grad.astype(bf16)
    key_b = key_grad.astype(bf16)
    value_gb = value_local.astype(bf16)
    act_one_grad = (
        jnp.dot(query_b, full_wq.T, preferred_element_type=f32)
        + jnp.dot(key_b, full_wk.T, preferred_element_type=f32)
        + jnp.dot(value_gb, full_wv.T, preferred_element_type=f32)
    )
    grad_gain_one = jnp.sum(act_one_grad * normed_one, axis=0)
    input_grad = residual_grad + rms_back(act_one_grad * gain_one, normed_one, inverse_one)

    sums = (
        jnp.sum(query_grad, axis=0),
        jnp.sum(key_grad, axis=0),
        jnp.sum(value_local, axis=0),
        grad_gain_one,
    )
    high, low = split_sum(jnp.concatenate([s.reshape(ctx_count, -1) for s in sums], 1))
    high_two, low_two = split_sum(grad_gain_two.reshape(ctx_count, -1))
    fill = ((0, 0), (0, wide - high_two.shape[1]))
    sum_rows = jnp.stack([high, low, jnp.pad(high_two, fill), jnp.pad(low_two, fill)], 1)
    sum_rows = jnp.pad(sum_rows, ((0, 0), (0, 12), (0, 0)))
    blocks = jnp.concatenate(
        [
            jnp.transpose(g.reshape(tokens, ctx_count, -1), (1, 0, 2))
            for g in (query_b, key_b, value_gb, residual_b)
        ],
        2,
    )
    columns = exchange(jnp.concatenate([blocks, sum_rows], 1), "ctx")
    column_sums = jnp.sum(columns[:, tokens : tokens + 4].astype(f32), axis=0)
    column_sums = jnp.stack(
        [column_sums[0] + column_sums[1], column_sums[2] + column_sums[3]], 0
    )
    columns = columns[:, :tokens].reshape(seq_length, wide)
    act_one_all = saved_all[:, :model]
    attended_all = saved_all[:, model:]
    split = q_cols + 2 * k_cols
    grad_in = jnp.dot(act_one_all.T, columns[:, :split], preferred_element_type=f32)
    grad_wo = jnp.dot(attended_all.T, columns[:, split:], preferred_element_type=f32)
    grads = jnp.concatenate([grad_in, grad_wo], 1).astype(bf16).reshape(data_count, -1, wide)
    high, low = split_sum(column_sums)
    sum_rows = jnp.pad(jnp.concatenate([high, low], 0), ((0, 12), (0, 0)))
    sum_rows = jnp.broadcast_to(sum_rows[None], (data_count,) + sum_rows.shape)
    final = jnp.sum(
        exchange(jnp.concatenate([grads, sum_rows], 1), "dp").astype(f32), axis=0
    )
    first_sums = final[in_rows] + final[in_rows + 2]
    second_sums = final[in_rows + 1] + final[in_rows + 3]
    return (
        output[None],
        input_grad[None],
        first_sums[split:],
        final[:in_rows, :q_cols],
        first_sums[:q_cols],
        final[:in_rows, q_cols : q_cols + k_cols],
        first_sums[q_cols : q_cols + k_cols],
        final[:in_rows, q_cols + k_cols : split],
        first_sums[q_cols + k_cols : split],
        final[:in_rows, split:],
        second_sums[: norm2_gain.shape[0]],
        gate_up_grad[:, :units],
        gate_up_grad[:, units:],
        down_grad,
    )


def solution(mesh):
    in_specs = (
        P("dp", "ctx", None),
        P("dp", "ctx"),
        P("dp", "ctx", None),
        P("ctx"),
        P("dp", "ctx"),
        P("ctx"),
        P("dp", "ctx"),
        P("ctx"),
        P("dp", "ctx"),
        P("ctx"),
        P("dp", "ctx"),
        P("ctx"),
        P("dp", "ctx"),
        P("dp", "ctx"),
        P("dp", "ctx"),
    )
    out_specs = (
        P("dp", "ctx", None),
        P("dp", "ctx", None),
        P("ctx"),
        P("dp", "ctx"),
        P("ctx"),
        P("dp", "ctx"),
        P("ctx"),
        P("dp", "ctx"),
        P("ctx"),
        P("dp", "ctx"),
        P("ctx"),
        P("dp", "ctx"),
        P("dp", "ctx"),
        P("dp", "ctx"),
    )
    return jax.shard_map(
        per_device, mesh=mesh, in_specs=in_specs, out_specs=out_specs, check_vma=False
    )
```

```python
import jax
import jax.numpy as jnp
from jax import lax
from jax.sharding import PartitionSpec as P

HEADS = 14
KV_HEADS = 2
HEAD = 64
GROUP = 7


EPSILON = 1e-06
THETA = 1000000.0


def rms_parts(values):
    inverse = lax.rsqrt(jnp.mean(values * values, axis=-1, keepdims=True) + EPSILON)
    return (values * inverse, inverse)


def rms_back(grads, normed, inverse):
    return inverse * (grads - normed * jnp.mean(grads * normed, axis=-1, keepdims=True))


def rotary(places):
    half_size = HEAD // 2
    freq = THETA ** (-(jnp.arange(half_size).astype(jnp.float32) * 2.0 / HEAD))
    angle = places.astype(jnp.float32)[:, None] * freq[None, :]
    cosine = jnp.cos(angle)
    sine = jnp.sin(angle)
    return (
        jnp.concatenate([cosine, cosine], 1)[:, None, :],
        jnp.concatenate([sine, sine], 1)[:, None, :],
    )


def turn_half(values):
    half_size = values.shape[-1] // 2
    return jnp.concatenate([-values[..., half_size:], values[..., :half_size]], axis=-1)


def rotate(values, cosine, sine):
    return values * cosine + turn_half(values) * sine


def unrotate(grads, cosine, sine):
    return grads * cosine - turn_half(grads) * sine


def gather(block, axes):
    return lax.all_gather(block, axes, axis=0, tiled=False)


def exchange(blocks, axis):
    return lax.all_to_all(blocks, axis, split_axis=0, concat_axis=0, tiled=True)


def summed_scatter(blocks, axis):
    return lax.psum_scatter(blocks, axis, scatter_dimension=0, tiled=False)


def attend_forward(queries, query_pos, keys_sorted, values_sorted, blocks, width, scaling):
    row_count, kv_count, group_size, head_size = queries.shape

    def advance(index_block, carry):
        running_max, running_sum, weighted = carry
        first = index_block * width
        block_keys = lax.dynamic_slice_in_dim(keys_sorted, first, width, 0)
        block_values = lax.dynamic_slice_in_dim(values_sorted, first, width, 0)
        key_pos = first + jnp.arange(width, dtype=jnp.int32)
        scores = (
            jnp.einsum("qkgd,skd->kgqs", queries, block_keys, preferred_element_type=jnp.float32)
            * scaling
        )
        scores = jnp.where(key_pos[None, :] <= query_pos[:, None], scores, -jnp.inf)
        new_max = jnp.maximum(running_max, jnp.max(scores, axis=-1))
        rescale = jnp.exp(running_max - new_max)
        exponent = jnp.exp(scores - new_max[..., None])
        running_sum = running_sum * rescale + jnp.sum(exponent, axis=-1)
        weighted = weighted * rescale[..., None] + jnp.einsum(
            "kgqs,skd->kgqd",
            exponent.astype(jnp.bfloat16),
            block_values,
            preferred_element_type=jnp.float32,
        )
        return (new_max, running_sum, weighted)

    start_state = (
        jnp.full((kv_count, group_size, row_count), -jnp.inf, jnp.float32),
        jnp.zeros((kv_count, group_size, row_count), jnp.float32),
        jnp.zeros((kv_count, group_size, row_count, head_size), jnp.float32),
    )
    running_max, running_sum, weighted = lax.fori_loop(0, blocks, advance, start_state)
    return (weighted / running_sum[..., None], running_max + jnp.log(running_sum))


def attend_backward(
    queries,
    query_pos,
    keys_sorted,
    values_sorted,
    grad_out,
    out_rows,
    log_total,
    blocks,
    width,
    scaling,
    key_grads,
    value_grads,
):
    delta_rows = jnp.sum(grad_out.astype(jnp.float32) * out_rows.astype(jnp.float32), axis=-1)

    def advance(index_block, carry):
        query_grad, key_acc, value_acc = carry
        first = index_block * width
        block_keys = lax.dynamic_slice_in_dim(keys_sorted, first, width, 0)
        block_values = lax.dynamic_slice_in_dim(values_sorted, first, width, 0)
        key_pos = first + jnp.arange(width, dtype=jnp.int32)
        scores = (
            jnp.einsum("qkgd,skd->kgqs", queries, block_keys, preferred_element_type=jnp.float32)
            * scaling
        )
        scores = jnp.where(key_pos[None, :] <= query_pos[:, None], scores, -jnp.inf)
        prob = jnp.exp(scores - log_total[..., None])
        value_part = jnp.einsum(
            "kgqs,kgqd->skd",
            prob.astype(jnp.bfloat16),
            grad_out,
            preferred_element_type=jnp.float32,
        )
        prob_grad = jnp.einsum(
            "kgqd,skd->kgqs", grad_out, block_values, preferred_element_type=jnp.float32
        )
        score_grad = (prob * (prob_grad - delta_rows[..., None]) * scaling).astype(jnp.bfloat16)
        query_grad = query_grad + jnp.einsum(
            "kgqs,skd->kgqd", score_grad, block_keys, preferred_element_type=jnp.float32
        )
        key_part = jnp.einsum(
            "kgqs,qkgd->skd", score_grad, queries, preferred_element_type=jnp.float32
        )
        key_acc = lax.dynamic_update_slice_in_dim(
            key_acc, lax.dynamic_slice_in_dim(key_acc, first, width, 0) + key_part, first, 0
        )
        value_acc = lax.dynamic_update_slice_in_dim(
            value_acc, lax.dynamic_slice_in_dim(value_acc, first, width, 0) + value_part, first, 0
        )
        return (query_grad, key_acc, value_acc)

    row_count, kv_count, group_size, head_size = queries.shape
    start_state = (
        jnp.zeros((kv_count, group_size, row_count, head_size), jnp.float32),
        key_grads,
        value_grads,
    )
    return lax.fori_loop(0, blocks, advance, start_state)


def permuted_gather(block, data_count, ctx_count):
    mine = lax.axis_index("dp")
    stacked = jnp.zeros((data_count,) + block.shape, block.dtype)
    stacked = lax.dynamic_update_index_in_dim(stacked, block, mine, 0)
    for turn in range(1, data_count):
        pairs = [(d, (d + turn) % data_count) for d in range(data_count)]
        arrived = lax.ppermute(block, "dp", pairs)
        source = lax.rem(mine - turn + data_count, data_count)
        stacked = lax.dynamic_update_index_in_dim(stacked, arrived, source, 0)
    return stacked


def permuted_scatter(blocks, data_count):
    mine = lax.axis_index("dp")
    total = lax.dynamic_index_in_dim(blocks, mine, 0, keepdims=False).astype(jnp.float32)
    for turn in range(1, data_count):
        pairs = [(d, (d + turn) % data_count) for d in range(data_count)]
        target = lax.rem(mine + turn, data_count)
        piece = lax.dynamic_index_in_dim(blocks, target, 0, keepdims=False)
        total = total + lax.ppermute(piece, "dp", pairs).astype(jnp.float32)
    return total


def rows_to_columns(w_down, data_count, ctx_count):
    ratio = ctx_count // data_count
    rows = w_down.shape[0] // ratio
    low = lax.rem(lax.axis_index("ctx"), ratio)
    arrived = []
    for turn in range(ratio):
        pairs = [
            (a * ctx_count + ratio * d + e, d * ctx_count + ratio * a + (e + turn) % ratio)
            for a in range(data_count)
            for d in range(data_count)
            for e in range(ratio)
        ]
        block = lax.rem(low + turn, ratio)
        piece = lax.dynamic_slice_in_dim(w_down, block * rows, rows, 0)
        arrived.append(lax.ppermute(piece, ("dp", "ctx"), pairs))
    stacked = jnp.stack(arrived, 0)
    order = lax.rem(low - jnp.arange(ratio, dtype=jnp.int32) + ratio, ratio)
    stacked = stacked[order]
    return jnp.transpose(stacked, (1, 0, 2)).reshape(rows, -1)


def columns_to_rows(grad, data_count, ctx_count):
    ratio = ctx_count // data_count
    rows, columns = grad.shape
    width = columns // ratio
    low = lax.rem(lax.axis_index("ctx"), ratio)
    arrived = []
    for turn in range(ratio):
        pairs = [
            (d * ctx_count + ratio * a + (e + turn) % ratio, a * ctx_count + ratio * d + e)
            for a in range(data_count)
            for d in range(data_count)
            for e in range(ratio)
        ]
        block = lax.rem(low - turn + ratio, ratio)
        piece = lax.dynamic_slice_in_dim(grad, block * width, width, 1)
        arrived.append(lax.ppermute(piece, ("dp", "ctx"), pairs))
    order = lax.rem(low + jnp.arange(ratio, dtype=jnp.int32), ratio)
    placed = jnp.zeros((ratio, rows, width), grad.dtype)
    for turn in range(ratio):
        placed = lax.dynamic_update_slice_in_dim(placed, arrived[turn][None], order[turn], 0)
    return placed.reshape(ratio * rows, width)


def split_sum(values):
    high = values.astype(jnp.bfloat16)
    low = (values - high.astype(jnp.float32)).astype(jnp.bfloat16)
    return high, low


def per_device(
    block_input,
    positions,
    cotangent,
    norm1_gain,
    w_query,
    b_query,
    w_key,
    b_key,
    w_value,
    b_value,
    w_out,
    norm2_gain,
    w_gate,
    w_up,
    w_down,
):
    f32 = jnp.float32
    bf16 = jnp.bfloat16
    tokens, model = block_input.shape[1:]
    half_rows = tokens // 2
    ctx_count = lax.axis_size("ctx")
    data_count = lax.axis_size("dp")
    run_count = 2 * ctx_count
    seq_length = tokens * ctx_count
    kv_width = KV_HEADS * HEAD
    scaling = HEAD ** (-0.5)
    inputs = block_input[0].astype(f32)
    place = positions[0]
    cot_local = cotangent[0]
    starts = place.reshape(2, half_rows)[:, 0]
    in_rows = w_query.shape[0]
    q_cols = w_query.shape[1]
    k_cols = w_key.shape[1]
    o_cols = w_out.shape[1]
    wide = q_cols + 2 * k_cols + o_cols
    runs_row = jnp.pad((starts // half_rows).astype(bf16), (0, wide - 2))
    gain_row = jnp.pad(norm2_gain, (0, wide - norm2_gain.shape[0]))
    vectors = jnp.stack(
        [jnp.concatenate([b_query, b_key, b_value, norm1_gain]), gain_row, runs_row]
    )
    vectors = jnp.pad(vectors, ((0, 13), (0, 0)))
    packed = jnp.concatenate(
        [jnp.concatenate([w_query, w_key, w_value, w_out], 1), vectors], 0
    )
    everything = gather(packed, ("dp", "ctx"))
    everything = everything.reshape(data_count, ctx_count, in_rows + 16, wide)

    def columns_of(lower, width):
        part = everything[:, :, :in_rows, lower : lower + width]
        return jnp.transpose(part, (0, 2, 1, 3)).reshape(data_count * in_rows, ctx_count * width)

    full_wq = columns_of(0, q_cols)
    full_wk = columns_of(q_cols, k_cols)
    full_wv = columns_of(q_cols + k_cols, k_cols)
    full_wo = columns_of(q_cols + 2 * k_cols, o_cols)
    data_index = lax.axis_index("dp")
    mine = lax.dynamic_index_in_dim(everything[:, :, in_rows:, :], data_index, 0, keepdims=False)
    full_bq = mine[:, 0, :q_cols].reshape(-1)
    full_bk = mine[:, 0, q_cols : q_cols + k_cols].reshape(-1)
    full_bv = mine[:, 0, q_cols + k_cols : q_cols + 2 * k_cols].reshape(-1)
    gain_one = mine[:, 0, q_cols + 2 * k_cols :].reshape(-1).astype(f32)
    gain_two = mine[:, 1, : norm2_gain.shape[0]].reshape(-1).astype(f32)
    ranking = mine[:, 2, :2].reshape(-1).astype(jnp.int32)

    gate_up = permuted_gather(
        jnp.concatenate([w_gate, w_up], 1), data_count, ctx_count
    ).reshape(model, -1)
    units = w_gate.shape[1]
    down_columns = rows_to_columns(w_down, data_count, ctx_count)
    cot_all = gather(cot_local, "ctx").reshape(seq_length, model)

    normed_one, inverse_one = rms_parts(inputs)
    act_one = (normed_one * gain_one).astype(bf16)
    queries = jnp.dot(act_one, full_wq, preferred_element_type=f32) + full_bq.astype(f32)
    keys = jnp.dot(act_one, full_wk, preferred_element_type=f32) + full_bk.astype(f32)
    values = jnp.dot(act_one, full_wv, preferred_element_type=f32) + full_bv.astype(f32)
    cosine, sine = rotary(place)
    query_rot = rotate(queries.reshape(tokens, HEADS, HEAD), cosine, sine).astype(bf16)
    key_rot = (
        rotate(keys.reshape(tokens, KV_HEADS, HEAD), cosine, sine)
        .astype(bf16)
        .reshape(tokens, kv_width)
    )
    value_b = values.astype(bf16)
    key_value, down_columns = lax.optimization_barrier(
        (jnp.concatenate([key_rot, value_b], 1), down_columns)
    )
    both_all = gather(key_value, "ctx")
    my_down = permuted_gather(down_columns, data_count, ctx_count)
    my_down = jnp.transpose(my_down, (1, 0, 2)).reshape(units, model)
    run_index = jnp.arange(run_count, dtype=jnp.int32)
    owners = jnp.sum(
        jnp.where(ranking[None, :] == run_index[:, None], run_index[None, :], 0), axis=1
    )
    both_sorted = both_all.reshape(run_count, half_rows, 2 * kv_width)[owners].reshape(
        seq_length, 2, KV_HEADS, HEAD
    )
    keys_sorted = both_sorted[:, 0]
    values_sorted = both_sorted[:, 1]
    pieces = []
    log_totals = []
    block_counts = []
    for index_run in range(2):
        lower = index_run * half_rows
        row_block = query_rot[lower : lower + half_rows].reshape(half_rows, KV_HEADS, GROUP, HEAD)
        blocks = starts[index_run] // tokens + 1
        mixed, log_total = attend_forward(
            row_block,
            place[lower : lower + half_rows],
            keys_sorted,
            values_sorted,
            blocks,
            tokens,
            scaling,
        )
        pieces.append(jnp.transpose(mixed, (2, 0, 1, 3)).reshape(half_rows, HEADS * HEAD))
        log_totals.append(log_total)
        block_counts.append(blocks)
    attended = jnp.concatenate(pieces, 0).astype(bf16)
    residual = inputs + jnp.dot(attended, full_wo, preferred_element_type=f32)
    normed_two, inverse_two = rms_parts(residual)
    act_two = (normed_two * gain_two).astype(bf16)
    act_one_all = gather(act_one, "ctx").reshape(seq_length, model)
    act_two, act_one_all, cot_all, gate_up, my_down = lax.optimization_barrier(
        (act_two, act_one_all, cot_all, gate_up, my_down)
    )
    my_gate = gate_up[:, :units]
    my_up = gate_up[:, units:]
    act_two_all = gather(act_two, "ctx").reshape(seq_length, model)

    gate = jnp.dot(act_two_all, my_gate, preferred_element_type=f32)
    up_proj = jnp.dot(act_two_all, my_up, preferred_element_type=f32)
    sigmoid_gate = jax.nn.sigmoid(gate)
    silu_gate = gate * sigmoid_gate
    hidden = (silu_gate * up_proj).astype(bf16)
    out_part = jnp.dot(hidden, my_down, preferred_element_type=f32).astype(bf16)
    hidden_grad = jnp.dot(cot_all, my_down.T, preferred_element_type=f32)
    gate_grad = (hidden_grad * up_proj * sigmoid_gate * (1.0 + gate * (1.0 - sigmoid_gate))).astype(
        bf16
    )
    up_grad = (hidden_grad * silu_gate).astype(bf16)
    act_part = (
        jnp.dot(gate_grad, my_gate.T, preferred_element_type=f32)
        + jnp.dot(up_grad, my_up.T, preferred_element_type=f32)
    ).astype(bf16)
    act_two_grad = summed_scatter(act_part.reshape(ctx_count, tokens, model), "ctx")
    out_blocks = exchange(out_part.reshape(ctx_count, tokens, model), "ctx")
    output = (residual + jnp.sum(out_blocks.astype(f32), axis=0)).astype(bf16)

    grad_gate = jnp.dot(act_two_all.T, gate_grad, preferred_element_type=f32).astype(bf16)
    grad_up = jnp.dot(act_two_all.T, up_grad, preferred_element_type=f32).astype(bf16)
    grad_down = jnp.dot(hidden.T, cot_all, preferred_element_type=f32).astype(bf16)
    gate_up_grad = jnp.concatenate([grad_gate, grad_up], 1).reshape(data_count, -1, 2 * units)
    down_grad = jnp.transpose(grad_down.reshape(units, data_count, -1), (1, 0, 2))
    act_two_grad, gate_up_grad, down_grad = lax.optimization_barrier(
        (act_two_grad, gate_up_grad, down_grad)
    )
    act_two_grad = act_two_grad.astype(f32)
    attended_all = gather(attended, "ctx").reshape(seq_length, HEADS * HEAD)
    gate_up_grad = summed_scatter(gate_up_grad, "dp").astype(f32)
    down_grad = permuted_scatter(down_grad, data_count).astype(bf16)
    down_grad = columns_to_rows(down_grad, data_count, ctx_count).astype(f32)

    grad_gain_two = jnp.sum(act_two_grad * normed_two, axis=0)
    residual_grad = cot_local.astype(f32) + rms_back(
        act_two_grad * gain_two, normed_two, inverse_two
    )
    residual_b = residual_grad.astype(bf16)
    attended_grad = jnp.dot(residual_b, full_wo.T, preferred_element_type=f32).astype(bf16)
    key_grads = jnp.zeros((seq_length, KV_HEADS, HEAD), f32)
    value_grads = jnp.zeros((seq_length, KV_HEADS, HEAD), f32)
    query_parts = []
    for index_run in range(2):
        lower = index_run * half_rows
        row_block = query_rot[lower : lower + half_rows].reshape(half_rows, KV_HEADS, GROUP, HEAD)
        grad_rows = jnp.transpose(
            attended_grad[lower : lower + half_rows].reshape(half_rows, KV_HEADS, GROUP, HEAD),
            (1, 2, 0, 3),
        )
        out_rows = jnp.transpose(
            attended[lower : lower + half_rows].reshape(half_rows, KV_HEADS, GROUP, HEAD),
            (1, 2, 0, 3),
        )
        query_grad, key_grads, value_grads = attend_backward(
            row_block,
            place[lower : lower + half_rows],
            keys_sorted,
            values_sorted,
            grad_rows,
            out_rows,
            log_totals[index_run],
            block_counts[index_run],
            tokens,
            scaling,
            key_grads,
            value_grads,
        )
        query_parts.append(jnp.transpose(query_grad, (2, 0, 1, 3)))
    slots = jnp.concatenate(
        [key_grads.reshape(seq_length, kv_width), value_grads.reshape(seq_length, kv_width)], 1
    )
    slots = slots.reshape(run_count, half_rows, 2 * kv_width)[ranking]
    slots = slots.astype(bf16).reshape(ctx_count, tokens, 2 * kv_width)
    both_local = jnp.sum(exchange(slots, "ctx").astype(f32), axis=0)
    key_local = both_local[:, :kv_width]
    value_local = both_local[:, kv_width:]
    query_grad = unrotate(
        jnp.concatenate(query_parts, 0).reshape(tokens, HEADS, HEAD), cosine, sine
    ).reshape(tokens, HEADS * HEAD)
    key_grad = unrotate(key_local.reshape(tokens, KV_HEADS, HEAD), cosine, sine).reshape(
        tokens, kv_width
    )
    query_b = query_grad.astype(bf16)
    key_b = key_grad.astype(bf16)
    value_gb = value_local.astype(bf16)
    act_one_grad = (
        jnp.dot(query_b, full_wq.T, preferred_element_type=f32)
        + jnp.dot(key_b, full_wk.T, preferred_element_type=f32)
        + jnp.dot(value_gb, full_wv.T, preferred_element_type=f32)
    )
    grad_gain_one = jnp.sum(act_one_grad * normed_one, axis=0)
    input_grad = residual_grad + rms_back(act_one_grad * gain_one, normed_one, inverse_one)

    sums = (
        jnp.sum(query_grad, axis=0),
        jnp.sum(key_grad, axis=0),
        jnp.sum(value_local, axis=0),
        grad_gain_one,
    )
    high, low = split_sum(jnp.concatenate([s.reshape(ctx_count, -1) for s in sums], 1))
    high_two, low_two = split_sum(grad_gain_two.reshape(ctx_count, -1))
    fill = ((0, 0), (0, wide - high_two.shape[1]))
    sum_rows = jnp.stack([high, low, jnp.pad(high_two, fill), jnp.pad(low_two, fill)], 1)
    sum_rows = jnp.pad(sum_rows, ((0, 0), (0, 12), (0, 0)))
    blocks = jnp.concatenate(
        [
            jnp.transpose(g.reshape(tokens, ctx_count, -1), (1, 0, 2))
            for g in (query_b, key_b, value_gb, residual_b)
        ],
        2,
    )
    blocks, attended_all = lax.optimization_barrier(
        (jnp.concatenate([blocks, sum_rows], 1), attended_all)
    )
    columns = exchange(blocks, "ctx")
    column_sums = jnp.sum(columns[:, tokens : tokens + 4].astype(f32), axis=0)
    column_sums = jnp.stack(
        [column_sums[0] + column_sums[1], column_sums[2] + column_sums[3]], 0
    )
    columns = columns[:, :tokens].reshape(seq_length, wide)
    split = q_cols + 2 * k_cols
    grad_in = jnp.dot(act_one_all.T, columns[:, :split], preferred_element_type=f32)
    grad_wo = jnp.dot(attended_all.T, columns[:, split:], preferred_element_type=f32)
    grads = jnp.concatenate([grad_in, grad_wo], 1).astype(bf16).reshape(data_count, -1, wide)
    high, low = split_sum(column_sums)
    sum_rows = jnp.pad(jnp.concatenate([high, low], 0), ((0, 12), (0, 0)))
    sum_rows = jnp.broadcast_to(sum_rows[None], (data_count,) + sum_rows.shape)
    final = jnp.sum(
        exchange(jnp.concatenate([grads, sum_rows], 1), "dp").astype(f32), axis=0
    )
    first_sums = final[in_rows] + final[in_rows + 2]
    second_sums = final[in_rows + 1] + final[in_rows + 3]
    return (
        output[None],
        input_grad[None],
        first_sums[split:],
        final[:in_rows, :q_cols],
        first_sums[:q_cols],
        final[:in_rows, q_cols : q_cols + k_cols],
        first_sums[q_cols : q_cols + k_cols],
        final[:in_rows, q_cols + k_cols : split],
        first_sums[q_cols + k_cols : split],
        final[:in_rows, split:],
        second_sums[: norm2_gain.shape[0]],
        gate_up_grad[:, :units],
        gate_up_grad[:, units:],
        down_grad,
    )


def solution(mesh):
    in_specs = (
        P("dp", "ctx", None),
        P("dp", "ctx"),
        P("dp", "ctx", None),
        P("ctx"),
        P("dp", "ctx"),
        P("ctx"),
        P("dp", "ctx"),
        P("ctx"),
        P("dp", "ctx"),
        P("ctx"),
        P("dp", "ctx"),
        P("ctx"),
        P("dp", "ctx"),
        P("dp", "ctx"),
        P("dp", "ctx"),
    )
    out_specs = (
        P("dp", "ctx", None),
        P("dp", "ctx", None),
        P("ctx"),
        P("dp", "ctx"),
        P("ctx"),
        P("dp", "ctx"),
        P("ctx"),
        P("dp", "ctx"),
        P("ctx"),
        P("dp", "ctx"),
        P("ctx"),
        P("dp", "ctx"),
        P("dp", "ctx"),
        P("dp", "ctx"),
    )
    return jax.shard_map(
        per_device, mesh=mesh, in_specs=in_specs, out_specs=out_specs, check_vma=False
    )
```
